512 devices in a mesh: row: 8 (over y), col: 16 (over z, core), rep: 4 (over x).
Axes of the slice: x: 4, y: 8, z: 8, core: 2. Of those that a mesh axis runs over, the one named last changes fastest.
Arguments:
- p_values: float32 [256, 4, 12, 128, 128], P(('row', 'col'), 'rep'), may hold values from -2.5 to 2.5
- p_cols: int32 [1024, 12], replicated, may hold values from 0 to 1023, as said below
- out_cols: int32 [1024, 8], P(('row', 'col')), may hold values from 0 to 1023, as said below
Outputs:
- square: float32 [1024, 8, 128, 128], P(('row', 'col', 'rep'))
The draws below stay inside these ranges and needn't reach their ends.
Inputs may be any that keep to these rules, and one draw needn't show every extreme that they name: `p_cols`: block row r names 12 distinct block columns c with r - 16 <= c < r + 16; its slots l * 3 to (l + 1) * 3 - 1 hold exactly the 3 columns that are congruent to l modulo 4. `out_cols`: block row r names 8 distinct block columns c with r - 16 <= c <= r + 16.
All inputs are finite; a program needn't handle non-finite values.
Results may differ from the reference program's by a relative error of at most 0.0003.
Values sent between devices are 32-bit elements; how exact they have to be, the bound alone decides.
No kernel may reach another device: no remote copies, remote signals or barrier semaphores. Data moves between devices by JAX's collectives and lax.ppermute only.
A program may use at most 64 MiB of HBM per device.

```python
import jax
import jax.numpy as jnp
from jax import lax

BS = 128
KL = 3
F = 8
LAYERS = 4
K = 12
NB = 1024
W = 16


def draw_p_cols(key, part):
    groups = K // KL
    reach_count = 2 * W // groups
    row_ids = jnp.arange(NB, dtype=jnp.int32)[:, None, None]
    residue = jnp.arange(groups, dtype=jnp.int32)[None, :, None]
    steps_ahead = jnp.arange(reach_count, dtype=jnp.int32)[None, None, :]
    lowest = row_ids - W
    candidate = lowest + jnp.mod(residue - lowest, groups) + groups * steps_ahead
    inside = (candidate >= 0) & (candidate < NB)
    scores = jax.random.randint(jax.random.fold_in(key, 11), (NB, groups, reach_count), 0, 1 << 20, dtype=jnp.int32) * reach_count + steps_ahead
    boundary = (candidate == 0) | (candidate == NB - 1)
    scores = scores + jnp.where(boundary, 1 << 28, 0).astype(jnp.int32)
    scores = jnp.where(inside, scores, -1 - steps_ahead)
    ranked, chosen = lax.top_k(scores, KL)
    columns = jnp.take_along_axis(jnp.broadcast_to(candidate, scores.shape), chosen, axis=2)
    return columns.reshape(NB, K).astype(jnp.int32)


def draw_out_cols(key, part):
    span = 2 * W + 1
    row_ids = jnp.arange(NB, dtype=jnp.int32)[:, None]
    offsets = jnp.arange(span, dtype=jnp.int32)[None, :]
    candidate = row_ids - W + offsets
    inside = (candidate >= 0) & (candidate < NB)
    scores = jax.random.randint(jax.random.fold_in(key, 23), (NB, span), 0, 1 << 20, dtype=jnp.int32) * span + offsets
    boundary = (candidate == 0) | (candidate == NB - 1)
    scores = scores + jnp.where(boundary, 1 << 28, 0).astype(jnp.int32)
    scores = jnp.where(inside, scores, -1 - offsets)
    ranked, chosen = lax.top_k(scores, F)
    columns = jnp.take_along_axis(jnp.broadcast_to(candidate, scores.shape), chosen, axis=1)
    return columns.astype(jnp.int32)


def block_levels(own_key, dims, cuts, least, largest):
    def one(dim, parts):
        steps = jax.random.uniform(jax.random.fold_in(jax.random.fold_in(own_key, 6), dim), (parts,), jnp.float32, least / len(cuts), largest / len(cuts))
        return jnp.repeat(jnp.exp(steps), dims[dim] // parts).reshape((-1,) + (1,) * (len(dims) - dim - 1))

    level = one(*cuts[0])
    for cut in cuts[1:]:
        level = level * one(*cut)
    return level


def scatter_about(stream_key, dims, deviation, most, split=(), held_as=jnp.bfloat16):
    level = block_levels(stream_key, dims, split, -0.22, 0.18) if split else 1.0
    result = jax.random.normal(stream_key, dims, jnp.float32) * deviation * level
    return jnp.minimum(jnp.maximum(result, -most), most).astype(held_as)


def setup_inputs(seed: int = 0) -> dict:
    key_list = jax.random.split(jax.random.key(seed), 4)
    p_values = scatter_about(key_list[0], (NB // LAYERS, LAYERS, K, BS, BS), 0.18, 2.5, ((0, 128), (1, 4)), jnp.float32)
    p_cols = draw_p_cols(jax.random.fold_in(key_list[3], 71), 0)
    out_cols = draw_out_cols(jax.random.fold_in(key_list[3], 71), 0)
    return dict(p_values=p_values, p_cols=p_cols, out_cols=out_cols)


HIGHEST = lax.Precision.HIGHEST


def reference(p_values, p_cols, out_cols):
    stored = p_values.reshape(NB, K, BS, BS)
    slot_ids = jnp.arange(K, dtype=jnp.int32)

    def one_row(row_index):
        row_cols = p_cols[row_index]
        wanted = out_cols[row_index]
        far_cols = p_cols[row_cols]
        matches = far_cols[:, None, :] == wanted[None, :, None]
        slot_index = jnp.sum(jnp.where(matches, slot_ids[None, None, :], 0), axis=2).astype(jnp.int32)
        present = jnp.any(matches, axis=2)
        picked = stored[row_cols[:, None], slot_index]
        picked = jnp.where(present[:, :, None, None], picked, jnp.zeros_like(picked))
        return jnp.einsum("sab,sfbc->fac", stored[row_index], picked, precision=HIGHEST)

    return lax.map(one_row, jnp.arange(NB, dtype=jnp.int32))
```

```python
import functools

import jax
import jax.numpy as jnp
from jax import lax
from jax.experimental import pallas as pl
from jax.experimental.pallas import tpu as pltpu
from jax.sharding import PartitionSpec as P

HALF = 64
SEG = ("row", "col")


def roll_half(x):
    return pltpu.roll(x, HALF, x.ndim - 1)


def left_lanes(shape):
    return lax.broadcasted_iota(jnp.int32, shape, len(shape) - 1) < HALF


def prepare_body(layer, own, half0, half1, part0, part1, part2, part3):
    pairs = half0.shape[1]
    layers = 4
    per_layer = part0.shape[1]
    for t in range(pairs):
        low, high = own[0, t], own[0, t + pairs]
        left = left_lanes(low.shape)
        half0[0, t] = jnp.where(left, low, roll_half(high))
        half1[0, t] = jnp.where(left, roll_half(low), high)
    for step, part in enumerate((part0, part1, part2, part3)):
        first = lax.rem(layer[0] + step, layers) * per_layer
        part[0] = own[0, pl.ds(first, per_layer)]


def prepare(layer, own):
    rows, slots, size, _ = own.shape
    pairs, per_layer = slots // 2, slots // 4
    half = jax.ShapeDtypeStruct((rows, pairs, size, size), own.dtype)
    part = jax.ShapeDtypeStruct((rows, per_layer, size, size), own.dtype)

    def spec(count):
        return pl.BlockSpec((1, count, size, size), lambda q, _: (q, 0, 0, 0))

    return pl.pallas_call(
        prepare_body,
        grid_spec=pltpu.PrefetchScalarGridSpec(
            num_scalar_prefetch=1,
            grid=(rows,),
            in_specs=[spec(slots)],
            out_specs=[spec(pairs)] * 2 + [spec(per_layer)] * 4,
        ),
        out_shape=[half] * 2 + [part] * 4,
        compiler_params=pltpu.CompilerParams(vmem_limit_bytes=24 << 20),
        cost_estimate=pl.CostEstimate(flops=0, transcendentals=0, bytes_accessed=5 << 20),
        name="prepare",
    )(layer, own)


def split(x):
    high = x.astype(jnp.bfloat16)
    return high, (x - high.astype(jnp.float32)).astype(jnp.bfloat16)


def product_body(where, layer, *refs):
    parts, windows, outs = refs[:4], refs[4:9], refs[9:13]
    a_high, a_low, w_high, w_low, p_high, p_low = refs[13:]
    rows, per_layer, size, _ = parts[0].shape
    pairs = windows[0].shape[1]
    slots = 2 * pairs
    layers = 4
    out_pairs = outs[0].shape[1]
    none = len(windows) * rows * slots

    for d, part in enumerate(parts):
        for q in range(rows):
            for s in range(per_layer):
                high, low = split(part[q, s])
                cols = slice(s * size, (s + 1) * size)
                a_high[d * rows + q, :, cols] = high
                a_low[d * rows + q, :, cols] = low

    def load_window(b, window):
        for q in range(rows):
            for t in range(pairs):
                x = window[q, t]
                base = (b * rows + q) * slots + t
                high, low = split(x)
                w_high[base], w_low[base] = high, low
                high, low = split(roll_half(x))
                w_high[base + pairs], w_low[base + pairs] = high, low

    for b, window in enumerate(windows):
        load_window(b, window)
    w_high[none] = jnp.zeros((size, size), jnp.bfloat16)
    w_low[none] = jnp.zeros((size, size), jnp.bfloat16)
    left = left_lanes((size, size))
    for d, out in enumerate(outs):
        for i in range(2):
            row = 2 * lax.rem(layer[0] + d, layers) + i
            entry = lax.rem(layer[0] + layers - lax.rem(row, layers), layers) * rows + lax.div(row, layers)
            for s in range(per_layer):
                at = (row * per_layer + s) * 2 * out_pairs
                for p in range(out_pairs):
                    one, two = where[at + p], where[at + out_pairs + p]
                    to = (slice(s * size, (s + 1) * size), slice(p * size, (p + 1) * size))
                    p_high[to] = jnp.where(left, w_high[one], w_high[two])
                    p_low[to] = jnp.where(left, w_low[one], w_low[two])
            dot = functools.partial(jnp.dot, preferred_element_type=jnp.float32)
            high = a_high[entry]
            total = dot(high, p_high[...]) + (dot(high, p_low[...]) + dot(a_low[entry], p_high[...]))
            for p in range(out_pairs):
                out[i, p] = total[:, p * size : (p + 1) * size]


def product(where, layer, parts, windows):
    rows, per_layer, size, _ = parts[0].shape
    pairs = windows[0].shape[1]
    slots = 2 * pairs
    out_pairs = 4
    vmem = pl.BlockSpec(memory_space=pltpu.VMEM)
    smem = pl.BlockSpec(memory_space=pltpu.SMEM)
    blocks = len(windows) * rows * slots + 1
    width = per_layer * size
    return pl.pallas_call(
        product_body,
        in_specs=[smem, smem] + [vmem] * 9,
        out_specs=[vmem] * 4,
        out_shape=[jax.ShapeDtypeStruct((2, out_pairs, size, size), jnp.float32)] * 4,
        scratch_shapes=[pltpu.VMEM((4 * rows, size, width), jnp.bfloat16)] * 2
        + [pltpu.VMEM((blocks, size, size), jnp.bfloat16)] * 2
        + [pltpu.VMEM((width, out_pairs * size), jnp.bfloat16)] * 2,
        compiler_params=pltpu.CompilerParams(vmem_limit_bytes=40 << 20),
        cost_estimate=pl.CostEstimate(flops=2_400_000_000, transcendentals=0, bytes_accessed=8 << 20),
        name="product",
    )(where, layer, *parts, *windows)


def gather_body(*refs):
    out = refs[-1]
    half0, half1 = refs[:4], refs[4:8]
    pairs = half0[0].shape[1]
    for p in range(pairs):
        one = (half0[0][0, p] + half0[1][0, p]) + (half0[2][0, p] + half0[3][0, p])
        two = (half1[0][0, p] + half1[1][0, p]) + (half1[2][0, p] + half1[3][0, p])
        left = left_lanes(one.shape)
        out[0, p] = jnp.where(left, one, roll_half(two))
        out[0, p + pairs] = jnp.where(left, roll_half(one), two)


def add_up(half0, half1):
    rows, pairs, size, _ = half0[0].shape
    spec = pl.BlockSpec((1, pairs, size, size), lambda i: (i, 0, 0, 0))
    return pl.pallas_call(
        gather_body,
        grid=(rows,),
        in_specs=[spec] * 8,
        out_specs=pl.BlockSpec((1, 2 * pairs, size, size), lambda i: (i, 0, 0, 0)),
        out_shape=jax.ShapeDtypeStruct((rows, 2 * pairs, size, size), jnp.float32),
        compiler_params=pltpu.CompilerParams(vmem_limit_bytes=24 << 20),
        cost_estimate=pl.CostEstimate(flops=0, transcendentals=0, bytes_accessed=5 << 20),
        name="add_up",
    )(*half0, *half1)


def find(p_cols, out_cols, segment, layer):
    seg_rows, out_count = out_cols.shape
    total_rows, slots = p_cols.shape
    per_layer = slots // 4
    span = 5 * seg_rows
    first = jnp.clip(segment * seg_rows - 2 * seg_rows, 0, total_rows - span)
    near = lax.dynamic_slice(p_cols, (first, 0), (span, slots))
    inner = lax.dynamic_slice(p_cols, (segment * seg_rows, layer * per_layer), (seg_rows, per_layer))
    at = jnp.arange(span, dtype=jnp.int32)[None, None, :, None]
    far = jnp.sum(jnp.where(inner[:, :, None, None] - first == at, near[None, None], 0), axis=2)
    matches = far[:, :, None, :] == out_cols[:, None, :, None]
    slot_ids = jnp.arange(slots, dtype=jnp.int32)
    slot = jnp.sum(jnp.where(matches, slot_ids + 1, 0), axis=3) - 1
    offset = inner // seg_rows - segment
    even = segment % 2 == 0
    sign = jnp.where(even, offset, -offset)
    source = jnp.where(sign == 0, 0, jnp.where(sign == 1, 1, jnp.where(sign == 2, 2, jnp.where(sign == -2, 3, 4))))
    base = (source * 2 + (inner // 4) % 2) * slots
    swapped = jnp.where(jnp.arange(out_count) < out_count // 2, 0, slots // 2)
    place = (slot + swapped) % slots
    none = 5 * 2 * slots
    return jnp.where(slot >= 0, base[:, :, None] + place, none).reshape(-1)


def on_device(p_values, p_cols, out_cols):
    layers = lax.axis_size("rep")
    layer = lax.axis_index("rep")
    segment = lax.axis_index(SEG)
    segments = lax.axis_size(SEG[0]) * lax.axis_size(SEG[1])
    own = p_values[:, 0]
    layer_ref = layer.reshape(1).astype(jnp.int32)

    def on_segments(x, step):
        pairs = [(i, step(i)) for i in range(segments) if 0 <= step(i) < segments]
        return lax.ppermute(x, SEG, pairs)

    def partner(x):
        return on_segments(x, lambda i: i ^ 1)

    def forwarded(x):
        return on_segments(x, lambda i: i - 2 if i % 2 == 0 else i + 2)

    def kept(x):
        return on_segments(x, lambda i: i + 2 if i % 2 == 0 else i - 2)

    def to_layer(x, step):
        return lax.ppermute(x, "rep", [(i, (i + step) % layers) for i in range(layers)])

    half0, half1, *mine = prepare(layer_ref, own)
    where = find(p_cols, out_cols, segment, layer)

    ahead0 = forwarded(half0)
    behind0 = kept(half0)
    parts = [mine[0]] + [to_layer(mine[step], step) for step in (1, 2, 3)]
    other0, other1 = partner(half0), partner(half1)
    across0 = partner(ahead0)
    half1_later, ahead0, behind0 = lax.optimization_barrier((half1, ahead0, behind0))
    ahead1 = forwarded(half1_later)
    behind1 = kept(half1_later)
    across1 = partner(ahead1)

    def sums(windows):
        shares = product(where, layer_ref, parts, windows)
        return [shares[0]] + [to_layer(shares[step], step) for step in (1, 2, 3)]

    sum0 = sums((half0, other0, ahead0, behind0, across0))
    sum1 = sums((half1, other1, ahead1, behind1, across1))
    return add_up(sum0, sum1)


def solution(mesh):
    in_specs = (P(("row", "col"), "rep", None, None, None), P(), P(("row", "col"), None))
    out_specs = P(("row", "col", "rep"), None, None, None)
    return jax.shard_map(
        on_device, mesh=mesh, in_specs=in_specs, out_specs=out_specs, check_vma=False
    )
```

```python
import functools

import jax
import jax.numpy as jnp
from jax import lax
from jax.experimental import pallas as pl
from jax.experimental.pallas import tpu as pltpu
from jax.sharding import PartitionSpec as P

HALF = 64
LAYERS = 4
ALL_ROWS = 1024
SEG = ("row", "col")
HBM = pl.BlockSpec(memory_space=pltpu.HBM)
VMEM = pl.BlockSpec(memory_space=pltpu.VMEM)
SMEM = pl.BlockSpec(memory_space=pltpu.SMEM)


def roll_half(x):
    return pltpu.roll(x, HALF, x.ndim - 1)


def left_lanes(size):
    return lax.broadcasted_iota(jnp.int32, (size, size), 1) < HALF


def pair(low, high, chunk, left):
    if chunk == 0:
        return jnp.where(left, low, roll_half(high))
    return jnp.where(left, roll_half(low), high)


def pair_rows(source, target, chunk):
    pairs = target.shape[0]
    left = left_lanes(source.shape[-1])
    for t in range(pairs):
        target[t] = pair(source[t], source[t + pairs], chunk, left)


def in_hbm(x):
    return pltpu.with_memory_space_constraint(x, pltpu.HBM)


def first_body(own, mine, half):
    rows, slots, _, _ = own.shape
    per_layer = slots // LAYERS
    for q in range(rows):
        for layer in range(LAYERS):
            mine[layer, q] = own[q, layer * per_layer : (layer + 1) * per_layer]
        pair_rows(own.at[q], half.at[q], 0)


def first(own):
    rows, slots, size, _ = own.shape
    mine, half = pl.pallas_call(
        first_body,
        in_specs=[VMEM],
        out_specs=[VMEM] * 2,
        out_shape=[
            jax.ShapeDtypeStruct((LAYERS, rows, slots // LAYERS, size, size), own.dtype),
            jax.ShapeDtypeStruct((rows, slots // 2, size, size), own.dtype),
        ],
        compiler_params=pltpu.CompilerParams(vmem_limit_bytes=12 << 20),
        cost_estimate=pl.CostEstimate(flops=0, transcendentals=0, bytes_accessed=3 << 20),
        name="first",
    )(own)
    return in_hbm(mine), in_hbm(half)


def later_body(own, other, other0, both1):
    for q in range(own.shape[0]):
        pair_rows(other.at[q], other0.at[q], 0)
        pair_rows(own.at[q], both1.at[0, q], 1)
        pair_rows(other.at[q], both1.at[1, q], 1)


def later(own, other):
    rows, slots, size, _ = own.shape
    half = (rows, slots // 2, size, size)
    return pl.pallas_call(
        later_body,
        in_specs=[VMEM] * 2,
        out_specs=[VMEM] * 2,
        out_shape=[jax.ShapeDtypeStruct(half, own.dtype), jax.ShapeDtypeStruct((2,) + half, own.dtype)],
        compiler_params=pltpu.CompilerParams(vmem_limit_bytes=12 << 20),
        cost_estimate=pl.CostEstimate(flops=0, transcendentals=0, bytes_accessed=5 << 20),
        name="later",
    )(own, other)


def second_body(both, out):
    out[...] = both[1]


def second(both):
    return pl.pallas_call(
        second_body,
        in_specs=[VMEM],
        out_specs=VMEM,
        out_shape=jax.ShapeDtypeStruct(both.shape[1:], both.dtype),
        compiler_params=pltpu.CompilerParams(vmem_limit_bytes=4 << 20),
        cost_estimate=pl.CostEstimate(flops=0, transcendentals=0, bytes_accessed=1 << 20),
        name="second",
    )(both)


def window_begin(segment, seg_rows):
    return jnp.clip(segment * seg_rows - 2 * seg_rows, 0, ALL_ROWS - 5 * seg_rows)


def find_body(segment_ref, layer_ref, near, out_cols, where):
    seg_rows, out_count = out_cols.shape
    slots, span = near.shape
    per_layer = slots // LAYERS
    rows = seg_rows // LAYERS
    segment, layer = segment_ref[0], layer_ref[0]
    begin = window_begin(segment, seg_rows)
    none = 5 * rows * slots
    odd = lax.rem(segment, 2)
    own_at = segment * seg_rows - begin

    @pl.loop(0, seg_rows)
    def _(row):
        wanted = [out_cols[row, f] for f in range(out_count)]
        for s in range(per_layer):
            inner = near[layer * per_layer + s, own_at + row]
            offset = lax.div(inner, seg_rows) - segment
            sign = jnp.where(odd == 1, -offset, offset)
            source = jnp.where(sign < 0, 4 + sign, jnp.where(sign == 2, 4, sign))
            base = (source * rows + lax.rem(lax.div(inner, LAYERS), rows)) * slots
            for f in range(out_count):
                group = lax.rem(wanted[f], LAYERS) * per_layer
                found = jnp.int32(none)
                for i in range(per_layer):
                    t = group + i
                    if f >= out_count // 2:
                        t = jnp.where(t < slots // 2, t + slots // 2, t - slots // 2)
                    found = jnp.where(near[group + i, inner - begin] == wanted[f], base + t, found)
                where[(row * per_layer + s) * out_count + f] = found


def find(segment, layer, near, out_cols):
    seg_rows, out_count = out_cols.shape
    count = seg_rows * (near.shape[0] // LAYERS) * out_count
    return pl.pallas_call(
        find_body,
        in_specs=[SMEM] * 4,
        out_specs=SMEM,
        out_shape=jax.ShapeDtypeStruct((count,), jnp.int32),
        cost_estimate=pl.CostEstimate(flops=0, transcendentals=0, bytes_accessed=1 << 20),
        name="find",
    )(segment, layer, near, out_cols)


def split(x):
    high = x.astype(jnp.bfloat16)
    return high, (x - high.astype(jnp.float32)).astype(jnp.bfloat16)


def entries_body(parts, a_high, a_low):
    _, rows, per_layer, size, _ = parts.shape
    for d in range(LAYERS):
        for q in range(rows):
            for s in range(per_layer):
                cols = slice(s * size, (s + 1) * size)
                high, low = split(parts[d, q, s])
                a_high[q * LAYERS + d, :, cols] = high
                a_low[q * LAYERS + d, :, cols] = low


def entries(parts):
    _, rows, per_layer, size, _ = parts.shape
    out = jax.ShapeDtypeStruct((LAYERS * rows, size, per_layer * size), jnp.bfloat16)
    return pl.pallas_call(
        entries_body,
        in_specs=[VMEM],
        out_specs=[VMEM] * 2,
        out_shape=[out] * 2,
        compiler_params=pltpu.CompilerParams(vmem_limit_bytes=12 << 20),
        cost_estimate=pl.CostEstimate(flops=0, transcendentals=0, bytes_accessed=3 << 20),
        name="entries",
    )(parts)


def product_body(spread, layer, where, a_high, a_low, *refs):
    count = len(refs) - (6 + (LAYERS if spread else 1))
    sources, outs, (out_v, w_high, w_low, p_high, p_low, sem) = refs[:count], refs[count:-6], refs[-6:]
    if not spread:
        outs = [outs[0].at[m] for m in range(LAYERS)]
    windows = []
    for ref in sources:
        windows += [ref] if len(ref.shape) == 4 else [ref.at[0], ref.at[1]]
    rows, pairs, size, _ = windows[0].shape
    slots = 2 * pairs
    out_pairs = out_v.shape[2]
    per_layer = slots // LAYERS
    none = len(windows) * rows * slots
    stores = [pltpu.make_async_copy(out_v.at[m], outs[m], sem.at[m]) for m in range(LAYERS)]
    w_high[none] = jnp.zeros((size, size), jnp.bfloat16)
    w_low[none] = jnp.zeros((size, size), jnp.bfloat16)
    for b, window in enumerate(windows):
        for q in range(rows):
            for t in range(pairs):
                x = window[q, t]
                base = (b * rows + q) * slots + t
                high, low = split(x)
                w_high[base], w_low[base] = high, low
                high, low = split(roll_half(x))
                w_high[base + pairs], w_low[base + pairs] = high, low
    left = left_lanes(size)
    dot = functools.partial(jnp.dot, preferred_element_type=jnp.float32)
    for at_row in range(a_high.shape[0]):
        i = at_row % 2
        owner = at_row // 2
        to_owner = (2, 1, 3, 0)[owner] if spread else owner
        row = 2 * lax.rem(layer[0] + to_owner, LAYERS) + i if spread else at_row
        for s in range(per_layer):
            at = (row * per_layer + s) * 2 * out_pairs
            for p in range(out_pairs):
                one, two = where[at + p], where[at + out_pairs + p]
                to = (i, slice(s * size, (s + 1) * size), slice(p * size, (p + 1) * size))
                p_high[to] = jnp.where(left, w_high[one], w_high[two])
                p_low[to] = jnp.where(left, w_low[one], w_low[two])
        high = a_high[row]
        total = dot(high, p_high[i]) + (dot(high, p_low[i]) + dot(a_low[row], p_high[i]))
        for p in range(out_pairs):
            out_v[to_owner, i, p] = total[:, p * size : (p + 1) * size]
        if i == 1:
            stores[to_owner].start()
    for store in stores:
        store.wait()


def product(spread, layer, where, a_high, a_low, *windows):
    rows, pairs, size, _ = windows[-1].shape
    width = a_high.shape[2]
    out_pairs = 4
    blocks = 5 * rows * 2 * pairs + 1
    out = jax.ShapeDtypeStruct((LAYERS, 2, out_pairs, size, size), jnp.float32)
    outs = [jax.ShapeDtypeStruct(out.shape[1:], out.dtype)] * LAYERS if spread else [out]
    shares = pl.pallas_call(
        functools.partial(product_body, spread),
        in_specs=[SMEM] * 2 + [VMEM] * (2 + len(windows)),
        out_specs=[HBM] * len(outs),
        out_shape=outs,
        scratch_shapes=[pltpu.VMEM(out.shape, out.dtype)]
        + [pltpu.VMEM((blocks, size, size), jnp.bfloat16)] * 2
        + [pltpu.VMEM((2, width, out_pairs * size), jnp.bfloat16)] * 2
        + [pltpu.SemaphoreType.DMA((LAYERS,))],
        compiler_params=pltpu.CompilerParams(vmem_limit_bytes=20 << 20),
        cost_estimate=pl.CostEstimate(flops=1 << 20, transcendentals=0, bytes_accessed=1 << 16),
        name="product_spread" if spread else "product",
    )(layer, where, a_high, a_low, *windows)
    return shares if spread else [in_hbm(share) for share in shares]


def add_first_body(shares, out):
    for i in range(out.shape[0]):
        for p in range(out.shape[1]):
            out[i, p] = (shares[0, i, p] + shares[1, i, p]) + (shares[2, i, p] + shares[3, i, p])


def add_first(shares):
    return pl.pallas_call(
        add_first_body,
        in_specs=[VMEM],
        out_specs=VMEM,
        out_shape=jax.ShapeDtypeStruct(shares.shape[1:], jnp.float32),
        compiler_params=pltpu.CompilerParams(vmem_limit_bytes=8 << 20),
        cost_estimate=pl.CostEstimate(flops=0, transcendentals=0, bytes_accessed=3 << 20),
        name="add_first",
    )(shares)


def add_last_body(half0, share0, share1, share2, share3, out):
    pairs = half0.shape[1]
    left = left_lanes(out.shape[-1])
    for p in range(pairs):
        one = half0[0, p]
        two = (share0[0, p] + share1[0, p]) + (share2[0, p] + share3[0, p])
        out[0, p] = jnp.where(left, one, roll_half(two))
        out[0, p + pairs] = jnp.where(left, roll_half(one), two)


def add_last(half0, shares):
    rows, pairs, size, _ = half0.shape
    spec = pl.BlockSpec((1, pairs, size, size), lambda i: (i, 0, 0, 0))
    return pl.pallas_call(
        add_last_body,
        grid=(rows,),
        in_specs=[spec] * 5,
        out_specs=pl.BlockSpec((1, 2 * pairs, size, size), lambda i: (i, 0, 0, 0)),
        out_shape=jax.ShapeDtypeStruct((rows, 2 * pairs, size, size), jnp.float32),
        compiler_params=pltpu.CompilerParams(vmem_limit_bytes=12 << 20),
        cost_estimate=pl.CostEstimate(flops=0, transcendentals=0, bytes_accessed=4 << 20),
        name="add_last",
    )(half0, *shares)


def on_device(p_values, p_cols, out_cols):
    layer = lax.axis_index("rep")
    segment = lax.axis_index(SEG)
    segments = lax.axis_size(SEG[0]) * lax.axis_size(SEG[1])
    seg_rows = out_cols.shape[0]
    own = p_values[:, 0]
    begin = window_begin(segment, seg_rows)
    segment_ref = segment.reshape(1).astype(jnp.int32)
    layer_ref = layer.reshape(1).astype(jnp.int32)

    def on_segments(x, step):
        pairs = [(i, step(i)) for i in range(segments) if 0 <= step(i) < segments]
        return lax.ppermute(x, SEG, pairs)

    def partner(x):
        return on_segments(x, lambda i: i ^ 1)

    def inward(x):
        return on_segments(x, lambda i: i - 2 if i % 2 == 0 else i + 2)

    def outward(x):
        return on_segments(x, lambda i: i + 2 if i % 2 == 0 else i - 2)

    def exchange(x):
        return lax.all_to_all(x, "rep", 0, 0, tiled=True)

    def to_layer(x, step):
        return lax.ppermute(x, "rep", [(i, (i + step) % LAYERS) for i in range(LAYERS)])

    near = lax.dynamic_slice(p_cols.T, (0, begin), (p_cols.shape[1], 5 * seg_rows))
    where = find(segment_ref, layer_ref, near, out_cols)
    mine, half0 = first(own)
    parts = exchange(mine)
    last0 = inward(half0)
    far0 = outward(half0)
    other = partner(own)
    last0, where = lax.optimization_barrier((last0, where))
    near0 = partner(last0)
    other0, here1 = later(own, other)
    here1, last0, far0, near0, parts, where = lax.optimization_barrier(
        (here1, last0, far0, near0, parts, where)
    )
    there1 = outward(here1)
    a_high, a_low = entries(parts)
    (shares0,) = product(False, layer_ref, where, a_high, a_low, half0, other0, far0, near0, last0)
    received0 = exchange(shares0)
    last1 = partner(there1[1])
    shares1 = product(True, layer_ref, where, a_high, a_low, here1, there1, last1)
    received0, kept1 = lax.optimization_barrier((received0, shares1[0]))
    received1 = [kept1] + [None] * 3
    for step in (2, 1, 3):
        received1[step] = to_layer(shares1[step], step)
    return add_last(add_first(received0), received1)


def solution(mesh):
    in_specs = (P(("row", "col"), "rep", None, None, None), P(), P(("row", "col"), None))
    out_specs = P(("row", "col", "rep"), None, None, None)
    return jax.shard_map(
        on_device, mesh=mesh, in_specs=in_specs, out_specs=out_specs, check_vma=False
    )
```

```python
import functools

import jax
import jax.numpy as jnp
from jax import lax
from jax.experimental import pallas as pl
from jax.experimental.pallas import tpu as pltpu
from jax.sharding import PartitionSpec as P

HALF = 64
LAYERS = 4
ALL_ROWS = 1024
SEG = ("row", "col")
HBM = pl.BlockSpec(memory_space=pltpu.HBM)
VMEM = pl.BlockSpec(memory_space=pltpu.VMEM)
SMEM = pl.BlockSpec(memory_space=pltpu.SMEM)


def turned(block, chunk):
    return block.T[chunk * HALF : (chunk + 1) * HALF]


def in_hbm(x):
    return pltpu.with_memory_space_constraint(x, pltpu.HBM)


def first_body(own, mine, half):
    rows, slots, _, _ = own.shape
    per_layer = slots // LAYERS
    for q in range(rows):
        for layer in range(LAYERS):
            mine[layer, q] = own[q, layer * per_layer : (layer + 1) * per_layer]
        for t in range(slots):
            half[q, t] = turned(own[q, t], 0)


def first(own):
    rows, slots, size, _ = own.shape
    mine, half = pl.pallas_call(
        first_body,
        in_specs=[VMEM],
        out_specs=[VMEM] * 2,
        out_shape=[
            jax.ShapeDtypeStruct((LAYERS, rows, slots // LAYERS, size, size), own.dtype),
            jax.ShapeDtypeStruct((rows, slots, HALF, size), own.dtype),
        ],
        compiler_params=pltpu.CompilerParams(vmem_limit_bytes=12 << 20),
        cost_estimate=pl.CostEstimate(flops=0, transcendentals=0, bytes_accessed=3 << 20),
        name="first",
    )(own)
    return in_hbm(mine), in_hbm(half)


def later_body(own, other, other0, both1):
    for q in range(own.shape[0]):
        for t in range(own.shape[1]):
            both1[0, q, t] = turned(own[q, t], 1)
            whole = other[q, t].T
            other0[q, t] = whole[:HALF]
            both1[1, q, t] = whole[HALF:]


def later(own, other):
    rows, slots, size, _ = own.shape
    half = (rows, slots, HALF, size)
    return pl.pallas_call(
        later_body,
        in_specs=[VMEM] * 2,
        out_specs=[VMEM] * 2,
        out_shape=[jax.ShapeDtypeStruct(half, own.dtype), jax.ShapeDtypeStruct((2,) + half, own.dtype)],
        compiler_params=pltpu.CompilerParams(vmem_limit_bytes=12 << 20),
        cost_estimate=pl.CostEstimate(flops=0, transcendentals=0, bytes_accessed=5 << 20),
        name="later",
    )(own, other)


def window_begin(segment, seg_rows):
    return jnp.clip(segment * seg_rows - 2 * seg_rows, 0, ALL_ROWS - 5 * seg_rows)


def find_body(segment_ref, layer_ref, near, out_cols, where):
    seg_rows, out_count = out_cols.shape
    slots, span = near.shape
    per_layer = slots // LAYERS
    rows = seg_rows // LAYERS
    segment, layer = segment_ref[0], layer_ref[0]
    begin = window_begin(segment, seg_rows)
    none = 5 * rows * slots
    odd = lax.rem(segment, 2)
    own_at = segment * seg_rows - begin

    @pl.loop(0, seg_rows)
    def _(row):
        wanted = [out_cols[row, f] for f in range(out_count)]
        for s in range(per_layer):
            inner = near[layer * per_layer + s, own_at + row]
            offset = lax.div(inner, seg_rows) - segment
            sign = jnp.where(odd == 1, -offset, offset)
            source = jnp.where(sign < 0, 4 + sign, jnp.where(sign == 2, 4, sign))
            base = (source * rows + lax.rem(lax.div(inner, LAYERS), rows)) * slots
            for f in range(out_count):
                group = lax.rem(wanted[f], LAYERS) * per_layer
                found = jnp.int32(none)
                for i in range(per_layer):
                    t = group + i
                    found = jnp.where(near[group + i, inner - begin] == wanted[f], base + t, found)
                where[(row * per_layer + s) * out_count + f] = found


def find(segment, layer, near, out_cols):
    seg_rows, out_count = out_cols.shape
    count = seg_rows * (near.shape[0] // LAYERS) * out_count
    return pl.pallas_call(
        find_body,
        in_specs=[SMEM] * 4,
        out_specs=SMEM,
        out_shape=jax.ShapeDtypeStruct((count,), jnp.int32),
        cost_estimate=pl.CostEstimate(flops=0, transcendentals=0, bytes_accessed=1 << 20),
        name="find",
    )(segment, layer, near, out_cols)


def split(x):
    high = x.astype(jnp.bfloat16)
    return high, (x - high.astype(jnp.float32)).astype(jnp.bfloat16)


def split_entries(parts, entry):
    _, rows, per_layer, size, _ = parts.shape
    for d in range(LAYERS):
        for q in range(rows):
            for s in range(per_layer):
                cols = slice(s * size, (s + 1) * size)
                high, low = split(parts[d, q, s])
                entry[q * LAYERS + d, :size, cols] = high
                entry[q * LAYERS + d, size:, cols] = low


def product_body(spread, layer, where, parts, *refs):
    count = len(refs) - (7 + (LAYERS if spread else 1))
    sources, outs, (out_v, entry, w_high, w_low, p_high, p_low, sem) = refs[:count], refs[count:-7], refs[-7:]
    if not spread:
        outs = [outs[0].at[m] for m in range(LAYERS)]
    windows = []
    for ref in sources:
        windows += [ref] if len(ref.shape) == 4 else [ref.at[0], ref.at[1]]
    rows, slots, _, size = windows[0].shape
    out_count = out_v.shape[2]
    per_layer = slots // LAYERS
    none = len(windows) * rows * slots
    stores = [pltpu.make_async_copy(out_v.at[m], outs[m], sem.at[m]) for m in range(LAYERS)]
    split_entries(parts, entry)
    w_high[none] = jnp.zeros((HALF, size), jnp.bfloat16)
    w_low[none] = jnp.zeros((HALF, size), jnp.bfloat16)
    for b, window in enumerate(windows):
        for q in range(rows):
            for t in range(slots):
                at = (b * rows + q) * slots + t
                w_high[at], w_low[at] = split(window[q, t])

    def dot(x, y):
        return lax.dot_general(x, y, (((1,), (1,)), ((), ())), preferred_element_type=jnp.float32)

    for at_row in range(entry.shape[0]):
        i = at_row % 2
        owner = at_row // 2
        to_owner = (2, 1, 3, 0)[owner] if spread else owner
        row = 2 * lax.rem(layer[0] + to_owner, LAYERS) + i if spread else at_row
        for s in range(per_layer):
            at = (row * per_layer + s) * out_count
            for f in range(out_count):
                found = where[at + f]
                to = (i, slice(f * HALF, (f + 1) * HALF), slice(s * size, (s + 1) * size))
                p_high[to] = w_high[found]
                p_low[to] = w_low[found]
        wide = dot(p_high[i], entry[row])
        total = wide[:, :size] + (wide[:, size:] + dot(p_low[i], entry[row, :size]))
        out_v[to_owner, i] = total.reshape(out_count, HALF, size)
        if i == 1:
            stores[to_owner].start()
    for store in stores:
        store.wait()


def product(spread, layer, where, parts, *windows):
    rows, slots, _, size = windows[-1].shape
    width = parts.shape[2] * size
    out_count = 8
    blocks = 5 * rows * slots + 1
    out = jax.ShapeDtypeStruct((LAYERS, 2, out_count, HALF, size), jnp.float32)
    outs = [jax.ShapeDtypeStruct(out.shape[1:], out.dtype)] * LAYERS if spread else [out]
    shares = pl.pallas_call(
        functools.partial(product_body, spread),
        in_specs=[SMEM] * 2 + [VMEM] * (1 + len(windows)),
        out_specs=[HBM] * len(outs),
        out_shape=outs,
        scratch_shapes=[
            pltpu.VMEM(out.shape, out.dtype),
            pltpu.VMEM((LAYERS * rows, 2 * size, width), jnp.bfloat16),
        ]
        + [pltpu.VMEM((blocks, HALF, size), jnp.bfloat16)] * 2
        + [pltpu.VMEM((2, out_count * HALF, width), jnp.bfloat16)] * 2
        + [pltpu.SemaphoreType.DMA((LAYERS,))],
        compiler_params=pltpu.CompilerParams(vmem_limit_bytes=(20 if spread else 60) << 20),
        cost_estimate=pl.CostEstimate(flops=1 << 20, transcendentals=0, bytes_accessed=1 << 16),
        name="product_spread" if spread else "product",
    )(layer, where, parts, *windows)
    return shares if spread else [in_hbm(share) for share in shares]


def add_first_body(shares, out):
    for i in range(out.shape[0]):
        for p in range(out.shape[1]):
            out[i, p] = (shares[0, i, p] + shares[1, i, p]) + (shares[2, i, p] + shares[3, i, p])


def add_first(shares):
    return pl.pallas_call(
        add_first_body,
        in_specs=[VMEM],
        out_specs=VMEM,
        out_shape=jax.ShapeDtypeStruct(shares.shape[1:], jnp.float32),
        compiler_params=pltpu.CompilerParams(vmem_limit_bytes=8 << 20),
        cost_estimate=pl.CostEstimate(flops=0, transcendentals=0, bytes_accessed=3 << 20),
        name="add_first",
    )(shares)


def add_last_body(half0, share0, share1, share2, share3, out):
    for f in range(half0.shape[1]):
        two = (share0[0, f] + share1[0, f]) + (share2[0, f] + share3[0, f])
        out[0, f] = jnp.concatenate([half0[0, f], two], axis=0).T


def add_last(half0, shares):
    rows, count, _, size = half0.shape
    spec = pl.BlockSpec((1, count, HALF, size), lambda i: (i, 0, 0, 0))
    return pl.pallas_call(
        add_last_body,
        grid=(rows,),
        in_specs=[spec] * 5,
        out_specs=pl.BlockSpec((1, count, size, size), lambda i: (i, 0, 0, 0)),
        out_shape=jax.ShapeDtypeStruct((rows, count, size, size), jnp.float32),
        compiler_params=pltpu.CompilerParams(vmem_limit_bytes=12 << 20),
        cost_estimate=pl.CostEstimate(flops=0, transcendentals=0, bytes_accessed=4 << 20),
        name="add_last",
    )(half0, *shares)


def on_device(p_values, p_cols, out_cols):
    layer = lax.axis_index("rep")
    segment = lax.axis_index(SEG)
    segments = lax.axis_size(SEG[0]) * lax.axis_size(SEG[1])
    seg_rows = out_cols.shape[0]
    own = p_values[:, 0]
    begin = window_begin(segment, seg_rows)
    segment_ref = segment.reshape(1).astype(jnp.int32)
    layer_ref = layer.reshape(1).astype(jnp.int32)

    def on_segments(x, step):
        pairs = [(i, step(i)) for i in range(segments) if 0 <= step(i) < segments]
        return lax.ppermute(x, SEG, pairs)

    def partner(x):
        return on_segments(x, lambda i: i ^ 1)

    def inward(x):
        return on_segments(x, lambda i: i - 2 if i % 2 == 0 else i + 2)

    def outward(x):
        return on_segments(x, lambda i: i + 2 if i % 2 == 0 else i - 2)

    def exchange(x):
        return lax.all_to_all(x, "rep", 0, 0, tiled=True)

    def to_layer(x, step):
        return lax.ppermute(x, "rep", [(i, (i + step) % LAYERS) for i in range(LAYERS)])

    near = lax.dynamic_slice(p_cols.T, (0, begin), (p_cols.shape[1], 5 * seg_rows))
    where = find(segment_ref, layer_ref, near, out_cols)
    mine, half0 = first(own)
    parts = exchange(mine)
    last0 = inward(half0)
    far0 = outward(half0)
    other = partner(own)
    last0, where = lax.optimization_barrier((last0, where))
    near0 = partner(last0)
    other0, here1 = later(own, other)
    here1, last0, far0, near0, parts, where = lax.optimization_barrier(
        (here1, last0, far0, near0, parts, where)
    )
    there1 = outward(here1)
    (shares0,) = product(False, layer_ref, where, parts, half0, other0, far0, near0, last0)
    received0 = exchange(shares0)
    last1 = partner(there1[1])
    shares1 = product(True, layer_ref, where, parts, here1, there1, last1)
    received0, kept1 = lax.optimization_barrier((received0, shares1[0]))
    received1 = [kept1] + [None] * 3
    for step in (2, 1, 3):
        received1[step] = to_layer(shares1[step], step)
    return add_last(add_first(received0), received1)


def solution(mesh):
    in_specs = (P(("row", "col"), "rep", None, None, None), P(), P(("row", "col"), None))
    out_specs = P(("row", "col", "rep"), None, None, None)
    return jax.shard_map(
        on_device, mesh=mesh, in_specs=in_specs, out_specs=out_specs, check_vma=False
    )
```

```python
import functools

import jax
import jax.numpy as jnp
from jax import lax
from jax.experimental import pallas as pl
from jax.experimental.pallas import tpu as pltpu
from jax.sharding import PartitionSpec as P

HALF = 64
LAYERS = 4
ALL_ROWS = 1024
SEG = ("row", "col")
HBM = pl.BlockSpec(memory_space=pltpu.HBM)
VMEM = pl.BlockSpec(memory_space=pltpu.VMEM)
SMEM = pl.BlockSpec(memory_space=pltpu.SMEM)


def turned(block, chunk):
    return block.T[chunk * HALF : (chunk + 1) * HALF]


def in_hbm(x):
    return pltpu.with_memory_space_constraint(x, pltpu.HBM)


def first_body(own, mine, half):
    rows, slots, _, _ = own.shape
    per_layer = slots // LAYERS
    for q in range(rows):
        for layer in range(LAYERS):
            mine[layer, q] = own[q, layer * per_layer : (layer + 1) * per_layer]
        for t in range(slots):
            half[q, t] = turned(own[q, t], 0)


def first(own):
    rows, slots, size, _ = own.shape
    mine, half = pl.pallas_call(
        first_body,
        in_specs=[VMEM],
        out_specs=[VMEM] * 2,
        out_shape=[
            jax.ShapeDtypeStruct((LAYERS, rows, slots // LAYERS, size, size), own.dtype),
            jax.ShapeDtypeStruct((rows, slots, HALF, size), own.dtype),
        ],
        compiler_params=pltpu.CompilerParams(vmem_limit_bytes=12 << 20),
        cost_estimate=pl.CostEstimate(flops=0, transcendentals=0, bytes_accessed=3 << 20),
        name="first",
    )(own)
    return in_hbm(mine), in_hbm(half)


def later_body(own, other, other0, both1):
    for q in range(own.shape[0]):
        for t in range(own.shape[1]):
            both1[0, q, t] = turned(own[q, t], 1)
            whole = other[q, t].T
            other0[q, t] = whole[:HALF]
            both1[1, q, t] = whole[HALF:]


def later(own, other):
    rows, slots, size, _ = own.shape
    half = (rows, slots, HALF, size)
    return pl.pallas_call(
        later_body,
        in_specs=[VMEM] * 2,
        out_specs=[VMEM] * 2,
        out_shape=[jax.ShapeDtypeStruct(half, own.dtype), jax.ShapeDtypeStruct((2,) + half, own.dtype)],
        compiler_params=pltpu.CompilerParams(vmem_limit_bytes=12 << 20),
        cost_estimate=pl.CostEstimate(flops=0, transcendentals=0, bytes_accessed=5 << 20),
        name="later",
    )(own, other)


def window_begin(segment, seg_rows):
    return jnp.clip(segment * seg_rows - 2 * seg_rows, 0, ALL_ROWS - 5 * seg_rows)


def find_body(segment_ref, layer_ref, near, out_cols, where):
    seg_rows, out_count = out_cols.shape
    slots, span = near.shape
    per_layer = slots // LAYERS
    rows = seg_rows // LAYERS
    segment, layer = segment_ref[0], layer_ref[0]
    begin = window_begin(segment, seg_rows)
    none = 5 * rows * slots
    odd = lax.rem(segment, 2)
    own_at = segment * seg_rows - begin

    @pl.loop(0, seg_rows)
    def _(row):
        wanted = [out_cols[row, f] for f in range(out_count)]
        for s in range(per_layer):
            inner = near[layer * per_layer + s, own_at + row]
            offset = lax.div(inner, seg_rows) - segment
            sign = jnp.where(odd == 1, -offset, offset)
            source = jnp.where(sign < 0, 4 + sign, jnp.where(sign == 2, 4, sign))
            base = (source * rows + lax.rem(lax.div(inner, LAYERS), rows)) * slots
            for f in range(out_count):
                group = lax.rem(wanted[f], LAYERS) * per_layer
                found = jnp.int32(none)
                for i in range(per_layer):
                    t = group + i
                    found = jnp.where(near[group + i, inner - begin] == wanted[f], base + t, found)
                where[(row * per_layer + s) * out_count + f] = found


def find(segment, layer, near, out_cols):
    seg_rows, out_count = out_cols.shape
    count = seg_rows * (near.shape[0] // LAYERS) * out_count
    return pl.pallas_call(
        find_body,
        in_specs=[SMEM] * 4,
        out_specs=SMEM,
        out_shape=jax.ShapeDtypeStruct((count,), jnp.int32),
        cost_estimate=pl.CostEstimate(flops=0, transcendentals=0, bytes_accessed=1 << 20),
        name="find",
    )(segment, layer, near, out_cols)


def split(x):
    high = x.astype(jnp.bfloat16)
    return high, (x - high.astype(jnp.float32)).astype(jnp.bfloat16)


def split_entries(parts, entry):
    _, rows, per_layer, size, _ = parts.shape
    for d in range(LAYERS):
        for q in range(rows):
            for s in range(per_layer):
                cols = slice(s * size, (s + 1) * size)
                high, low = split(parts[d, q, s])
                entry[q * LAYERS + d, :size, cols] = high
                entry[q * LAYERS + d, size:, cols] = low


def product_body(spread, layer, where, parts, *refs):
    count = len(refs) - (7 + (LAYERS if spread else 1))
    sources, outs, (out_v, entry, w_high, w_low, p_high, p_low, sem) = refs[:count], refs[count:-7], refs[-7:]
    if not spread:
        outs = [outs[0].at[m] for m in range(LAYERS)]
    windows = []
    for ref in sources:
        windows += [ref] if len(ref.shape) == 4 else [ref.at[0], ref.at[1]]
    rows, slots, _, size = windows[0].shape
    out_count = out_v.shape[2]
    per_layer = slots // LAYERS
    none = len(windows) * rows * slots
    stores = [pltpu.make_async_copy(out_v.at[m], outs[m], sem.at[m]) for m in range(LAYERS)]
    split_entries(parts, entry)
    w_high[none] = jnp.zeros((HALF, size), jnp.bfloat16)
    w_low[none] = jnp.zeros((HALF, size), jnp.bfloat16)
    for b, window in enumerate(windows):
        for q in range(rows):
            for t in range(slots):
                at = (b * rows + q) * slots + t
                w_high[at], w_low[at] = split(window[q, t])

    def dot(x, y):
        return lax.dot_general(x, y, (((1,), (1,)), ((), ())), preferred_element_type=jnp.float32)

    for at_row in range(entry.shape[0]):
        i = at_row % 2
        owner = at_row // 2
        to_owner = (2, 1, 3, 0)[owner] if spread else owner
        row = 2 * lax.rem(layer[0] + to_owner, LAYERS) + i if spread else at_row
        for s in range(per_layer):
            at = (row * per_layer + s) * out_count
            for f in range(out_count):
                found = where[at + f]
                to = (i, slice(f * HALF, (f + 1) * HALF), slice(s * size, (s + 1) * size))
                p_high[to] = w_high[found]
                p_low[to] = w_low[found]
        wide = dot(p_high[i], entry[row])
        total = wide[:, :size] + (wide[:, size:] + dot(p_low[i], entry[row, :size]))
        out_v[to_owner, i] = total.reshape(out_count, HALF, size)
        if i == 1:
            stores[to_owner].start()
    for store in stores:
        store.wait()


def product(spread, layer, where, parts, *windows):
    rows, slots, _, size = windows[-1].shape
    width = parts.shape[2] * size
    out_count = 8
    blocks = 5 * rows * slots + 1
    out = jax.ShapeDtypeStruct((LAYERS, 2, out_count, HALF, size), jnp.float32)
    outs = [jax.ShapeDtypeStruct(out.shape[1:], out.dtype)] * LAYERS if spread else [out]
    shares = pl.pallas_call(
        functools.partial(product_body, spread),
        in_specs=[SMEM] * 2 + [VMEM] * (1 + len(windows)),
        out_specs=[HBM] * len(outs),
        out_shape=outs,
        scratch_shapes=[
            pltpu.VMEM(out.shape, out.dtype),
            pltpu.VMEM((LAYERS * rows, 2 * size, width), jnp.bfloat16),
        ]
        + [pltpu.VMEM((blocks, HALF, size), jnp.bfloat16)] * 2
        + [pltpu.VMEM((2, out_count * HALF, width), jnp.bfloat16)] * 2
        + [pltpu.SemaphoreType.DMA((LAYERS,))],
        compiler_params=pltpu.CompilerParams(vmem_limit_bytes=(20 if spread else 60) << 20),
        cost_estimate=pl.CostEstimate(flops=1 << 20, transcendentals=0, bytes_accessed=1 << 16),
        name="product_spread" if spread else "product",
    )(layer, where, parts, *windows)
    return shares if spread else [in_hbm(share) for share in shares]


def add_first_body(shares, out):
    for i in range(out.shape[0]):
        for p in range(out.shape[1]):
            out[i, p] = (shares[0, i, p] + shares[1, i, p]) + (shares[2, i, p] + shares[3, i, p])


def add_first(shares):
    return pl.pallas_call(
        add_first_body,
        in_specs=[VMEM],
        out_specs=VMEM,
        out_shape=jax.ShapeDtypeStruct(shares.shape[1:], jnp.float32),
        compiler_params=pltpu.CompilerParams(vmem_limit_bytes=8 << 20),
        cost_estimate=pl.CostEstimate(flops=0, transcendentals=0, bytes_accessed=3 << 20),
        name="add_first",
    )(shares)


def add_last_body(half0, share0, share1, share2, share3, out):
    for f in range(half0.shape[1]):
        two = (share0[0, f] + share1[0, f]) + (share2[0, f] + share3[0, f])
        out[0, f] = jnp.concatenate([half0[0, f], two], axis=0).T


def add_last(half0, shares):
    rows, count, _, size = half0.shape
    spec = pl.BlockSpec((1, count, HALF, size), lambda i: (i, 0, 0, 0))
    return pl.pallas_call(
        add_last_body,
        grid=(rows,),
        in_specs=[spec] * 5,
        out_specs=pl.BlockSpec((1, count, size, size), lambda i: (i, 0, 0, 0)),
        out_shape=jax.ShapeDtypeStruct((rows, count, size, size), jnp.float32),
        compiler_params=pltpu.CompilerParams(vmem_limit_bytes=12 << 20),
        cost_estimate=pl.CostEstimate(flops=0, transcendentals=0, bytes_accessed=4 << 20),
        name="add_last",
    )(half0, *shares)


def on_device(p_values, p_cols, out_cols):
    layer = lax.axis_index("rep")
    segment = lax.axis_index(SEG)
    segments = lax.axis_size(SEG[0]) * lax.axis_size(SEG[1])
    seg_rows = out_cols.shape[0]
    own = p_values[:, 0]
    begin = window_begin(segment, seg_rows)
    segment_ref = segment.reshape(1).astype(jnp.int32)
    layer_ref = layer.reshape(1).astype(jnp.int32)

    def on_segments(x, step):
        pairs = [(i, step(i)) for i in range(segments) if 0 <= step(i) < segments]
        return lax.ppermute(x, SEG, pairs)

    def partner(x):
        return on_segments(x, lambda i: i ^ 1)

    def inward(x):
        return on_segments(x, lambda i: i - 2 if i % 2 == 0 else i + 2)

    def outward(x):
        return on_segments(x, lambda i: i + 2 if i % 2 == 0 else i - 2)

    def exchange(x):
        return lax.all_to_all(x, "rep", 0, 0, tiled=True)

    def to_layer(x, step):
        return lax.ppermute(x, "rep", [(i, (i + step) % LAYERS) for i in range(LAYERS)])

    near = lax.dynamic_slice(p_cols.T, (0, begin), (p_cols.shape[1], 5 * seg_rows))
    where = find(segment_ref, layer_ref, near, out_cols)
    mine, half0 = first(own)
    parts = exchange(mine)
    last0 = inward(half0)
    far0 = outward(half0)
    other = partner(own)
    last0, where = lax.optimization_barrier((last0, where))
    near0 = partner(last0)
    other0, here1 = later(own, other)
    here1, last0, far0, near0, parts, where = lax.optimization_barrier(
        (here1, last0, far0, near0, parts, where)
    )
    there1 = outward(here1)
    (shares0,) = product(False, layer_ref, where, parts, half0, other0, far0, near0, last0)
    received0 = exchange(shares0)
    last1 = partner(there1[1])
    shares1 = product(True, layer_ref, where, parts, here1, there1, last1)
    received0, kept1 = lax.optimization_barrier((received0, shares1[0]))
    received1 = [kept1] + [None] * 3
    for step in (2, 1, 3):
        received1[step] = to_layer(shares1[step], step)
    return add_last(add_first(received0), [received1[step] for step in (0, 2, 1, 3)])


def solution(mesh):
    in_specs = (P(("row", "col"), "rep", None, None, None), P(), P(("row", "col"), None))
    out_specs = P(("row", "col", "rep"), None, None, None)
    return jax.shard_map(
        on_device, mesh=mesh, in_specs=in_specs, out_specs=out_specs, check_vma=False
    )
```
